32 devices in a mesh: groups: 2 (over y), ctx: 16 (over z, x, core).
Axes of the slice: x: 2, y: 2, z: 4, core: 2. Of those that a mesh axis runs over, the one named last changes fastest.
Arguments:
- lookup_whole_numbers: int32 [16384, 512], P(('groups', 'ctx')), parts along dimension 0, may hold values from -127 to 127
- lookup_span_factors: float32 [256, 4], P(('groups', 'ctx')), parts along dimension 0, may hold values from 0.004 to 0.4
- payload_whole_numbers: int32 [16384, 512], P(('groups', 'ctx')), parts along dimension 0, may hold values from -127 to 127
- payload_span_factors: float32 [256, 4], P(('groups', 'ctx')), parts along dimension 0, may hold values from 0.004 to 0.03
- seed_means: bfloat16 [8, 1024, 128], P('groups'), parts along dimension 0, may hold values from -64 to 64
- softness_per_head: float32 [8], P('groups'), parts along dimension 0, may hold values from 8 to 40
- question_vectors: bfloat16 [2048, 2048], P(('groups', 'ctx')), parts along dimension 0, may hold values from -8 to 8
- final_projection_matrix: bfloat16 [2048, 4096], P('ctx'), may hold values from -0.125 to 0.125
Outputs:
- projected: bfloat16 [2048, 4096], P(('groups', 'ctx')), parts along dimension 0
The draws below stay inside these ranges and needn't reach their ends.
There are 2 independent parts, one for each index of `groups`. The reference program is written for one: setup_inputs(seed, part) draws one part's arguments, and reference() takes and returns one part's arrays. A program takes and returns all parts, laid end to end along the dimension named above; an argument that names none is the same for every part. Nothing has to cross between parts.
All inputs are finite; a program needn't handle non-finite values.
Results may differ from the reference program's by a relative error of at most 0.024.
Values may be sent and summed in bfloat16 or wider, within the bound.
A program may use at most 128 MiB of HBM per device.

```python
import math
import jax
import jax.numpy as jnp
from jax import lax

HEAD = 128
KVH = 4
QH = 16
D = 4096
NC = 1024
KB = 64
CTX_DEV = 512
Q_DEV = 64
CTX = 8192
QTOK = 1024
N_CTX = 16


aim_strength = 14.0


seed_factor = 1.27


def cluster_ids(key):
    devices_count = CTX // CTX_DEV
    share = NC // devices_count
    rows = jnp.arange(CTX, dtype=jnp.int32)
    own_block = (rows // CTX_DEV + devices_count // 2) % devices_count
    pick = jax.random.randint(jax.random.fold_in(key, 110), (CTX,), 0, 2, dtype=jnp.int32)
    inner = jax.random.randint(jax.random.fold_in(key, 111), (CTX,), 0, share, dtype=jnp.int32)
    anywhere = jax.random.randint(jax.random.fold_in(key, 112), (CTX,), 0, NC, dtype=jnp.int32)
    return jnp.where(pick == 1, own_block * share + inner, anywhere)


def templates(key, salt):
    return jax.random.randint(jax.random.fold_in(key, salt), (NC, KVH * HEAD), -100, 101, dtype=jnp.int32)


def clustered_codes(key, salt):
    ids = cluster_ids(key)
    noise = jax.random.randint(jax.random.fold_in(key, salt + 1), (CTX, KVH * HEAD), -20, 21, dtype=jnp.int32)
    return jnp.clip(jnp.take(templates(key, salt), ids, axis=0) + noise, -127, 127)


def shared_codes(key):
    return clustered_codes(key, 120)


def joint_softness(key):
    drawn = jax.random.uniform(jax.random.fold_in(key, 102), (KVH,), jnp.float32, math.log(8.0), math.log(40.0))
    return jnp.clip(jnp.exp(drawn), 8.0, 40.0)


def shared_scales(key):
    drawn = jax.random.uniform(jax.random.fold_in(key, 103), (CTX // KB, KVH), jnp.float32, math.log(0.02), math.log(0.06))
    return jnp.clip(jnp.exp(drawn), 0.004, 0.4)


def draw_lookup_whole_numbers(key, part):
    return shared_codes(key)


def draw_payload_whole_numbers(key, part):
    return clustered_codes(key, 130)


def draw_lookup_span_factors(key, part):
    return shared_scales(key)


def draw_softness_per_head(key, part):
    return joint_softness(key)


def draw_seed_means(key, part):
    base = templates(key, 120).astype(jnp.float32).reshape(NC, KVH, HEAD).transpose(1, 0, 2)
    roughness = jax.random.truncated_normal(jax.random.fold_in(key, 104), -6.0, 6.0, (KVH, NC, HEAD), jnp.float32)
    group_means = base * (seed_factor / HEAD) + 0.3 * roughness
    group_means = jnp.clip(group_means, -64.0, 64.0)
    return group_means.astype(jnp.bfloat16)


def draw_question_vectors(key, part):
    filled = jax.random.truncated_normal(jax.random.fold_in(key, 105), -6.0, 6.0, (QTOK, QH * HEAD), jnp.float32)
    devices_count = CTX // CTX_DEV
    share = NC // devices_count
    group_len = QH // KVH
    table = templates(key, 120).astype(jnp.float32).reshape(NC, KVH, HEAD)
    unit = table / jnp.sqrt(jnp.sum(table * table, axis=2, keepdims=True) + 1.0)
    rows = jnp.arange(QTOK, dtype=jnp.int32)
    device_of_row = rows // Q_DEV
    aims = []
    for query_head in range(QH):
        cluster = device_of_row * share + (rows + query_head) % share
        aims.append(jnp.take(unit[:, query_head // group_len], cluster, axis=0))
    filled = jnp.clip(filled + aim_strength * jnp.concatenate(aims, axis=1), -8.0, 8.0)
    return filled.astype(jnp.bfloat16)


def block_levels(key, extent, split, least, top_value):
    factor_of, own = 1.0, jax.random.fold_in(key, 6)
    for dim, blocks in split:
        draws = jnp.exp(jax.random.uniform(jax.random.fold_in(own, dim), (blocks,), jnp.float32, least / len(split), top_value / len(split)))
        factor_of = factor_of * jnp.repeat(draws, extent[dim] // blocks).reshape([-1 if axis == dim else 1 for axis in range(len(extent))])
    return factor_of


def normal_values(own_key, extent, spread, most, split=(), held_as=jnp.bfloat16):
    array = jax.random.normal(own_key, extent, jnp.float32) * spread
    if len(split) > 0:
        array = block_levels(own_key, extent, split, -0.22, 0.18) * array
    return jnp.clip(array, min=-most, max=most).astype(held_as)


def setup_inputs(seed: int = 0, part: int = 0) -> dict:
    keys = jax.random.split(jax.random.key(seed), 9)
    part_splits = jax.random.split(jax.random.fold_in(keys[8], part), 9)
    lookup_whole_numbers = draw_lookup_whole_numbers(jax.random.fold_in(jax.random.fold_in(keys[8], part), 71), part)
    lookup_span_factors = draw_lookup_span_factors(jax.random.fold_in(jax.random.fold_in(keys[8], part), 71), part)
    payload_whole_numbers = draw_payload_whole_numbers(jax.random.fold_in(jax.random.fold_in(keys[8], part), 71), part)
    payload_span_factors = jnp.clip(jnp.exp(math.log(0.03) - 2.014903 * jax.random.uniform(part_splits[3], (CTX // KB, KVH), jnp.float32) ** block_levels(part_splits[3], (CTX // KB, KVH), ((0, 16),), -0.2, 0.2)), 0.004, 0.03)
    seed_means = draw_seed_means(jax.random.fold_in(jax.random.fold_in(keys[8], part), 71), part)
    softness_per_head = draw_softness_per_head(jax.random.fold_in(jax.random.fold_in(keys[8], part), 71), part)
    question_vectors = draw_question_vectors(jax.random.fold_in(jax.random.fold_in(keys[8], part), 71), part)
    final_projection_matrix = normal_values(keys[7], (QH * HEAD, D), (QH * HEAD) ** -0.5, 0.125, ((0, 16),))
    return dict(lookup_whole_numbers=lookup_whole_numbers, lookup_span_factors=lookup_span_factors, payload_whole_numbers=payload_whole_numbers, payload_span_factors=payload_span_factors, seed_means=seed_means, softness_per_head=softness_per_head, question_vectors=question_vectors, final_projection_matrix=final_projection_matrix)


def dequantize(codes, scales, block_len):
    total_rows = codes.shape[0]
    heads_count = scales.shape[1]
    head_len = codes.shape[1] // heads_count
    scaled = codes.astype(jnp.float32).reshape(total_rows // block_len, block_len, heads_count, head_len)
    scaled = scaled * scales[:, None, :, None]
    return scaled.reshape(total_rows, heads_count, head_len).astype(jnp.bfloat16)

def smoothed_powers(lookup_word_lines, payload_word_lines, group_means, softness_amount):
    centre_f = group_means.astype(jnp.float32)
    power_two_entries = lax.optimization_barrier(jnp.sum(centre_f * centre_f, axis=1))
    raw_affinities = (2.0 * jnp.dot(lookup_word_lines, group_means.T, preferred_element_type=jnp.float32) - power_two_entries[None, :]) / softness_amount
    weights = jax.nn.softmax(raw_affinities, axis=1)
    rounded = weights.astype(jnp.bfloat16)
    dims = (((0,), (0,)), ((), ()))
    key_cluster_sums = lax.dot_general(rounded, lookup_word_lines, dims, preferred_element_type=jnp.float32)
    value_cluster_sums = lax.dot_general(rounded, payload_word_lines, dims, preferred_element_type=jnp.float32)
    member_counts = lax.optimization_barrier(jnp.sum(weights, axis=0))
    return (key_cluster_sums, value_cluster_sums, member_counts)

def attend(question_vectors, key_centres, value_centres, log_mass):
    rows_count = question_vectors.shape[0]
    heads_count = key_centres.shape[0]
    head_len = key_centres.shape[2]
    group_len = question_vectors.shape[1] // (heads_count * head_len)
    shaped = question_vectors.reshape(rows_count, heads_count, group_len, head_len)
    results = []
    for group_number in range(heads_count):
        query_rows = shaped[:, group_number].reshape(rows_count * group_len, head_len)
        scores = jnp.dot(query_rows, key_centres[group_number].T, preferred_element_type=jnp.float32)
        scores = scores / jnp.sqrt(jnp.float32(head_len)) + log_mass[group_number].astype(jnp.float32)[None, :]
        probs = jax.nn.softmax(scores, axis=1).astype(jnp.bfloat16)
        mixed = jnp.dot(probs, value_centres[group_number], preferred_element_type=jnp.float32).astype(jnp.bfloat16)
        results.append(mixed.reshape(rows_count, group_len * head_len))
    return jnp.concatenate(results, axis=1)

def reference(lookup_whole_numbers, lookup_span_factors, payload_whole_numbers, payload_span_factors, seed_means, softness_per_head, question_vectors, final_projection_matrix):
    lookup_word_lines = dequantize(lookup_whole_numbers, lookup_span_factors, KB).reshape(N_CTX, CTX_DEV, KVH, HEAD)
    payload_word_lines = dequantize(payload_whole_numbers, payload_span_factors, KB).reshape(N_CTX, CTX_DEV, KVH, HEAD)

    def totals(group_means):

        def accumulate(running, token_block):
            lookup_piece_lines, payload_piece_lines = token_block
            key_acc, value_acc, count_acc = running
            key_list, value_list, count_list = ([], [], [])
            for group_number in range(KVH):
                raised_powers = smoothed_powers(lookup_piece_lines[:, group_number], payload_piece_lines[:, group_number], group_means[group_number], softness_per_head[group_number])
                key_list.append(raised_powers[0])
                value_list.append(raised_powers[1])
                count_list.append(raised_powers[2])
            return ((key_acc + jnp.stack(key_list), value_acc + jnp.stack(value_list), count_acc + jnp.stack(count_list)), None)
        start_state = (jnp.zeros((KVH, NC, HEAD), jnp.float32), jnp.zeros((KVH, NC, HEAD), jnp.float32), jnp.zeros((KVH, NC), jnp.float32))
        final_state, discarded_item = lax.scan(accumulate, start_state, (lookup_word_lines, payload_word_lines))
        return final_state
    key_cluster_sums, unused_values, member_counts = totals(seed_means)
    solitary_means = ((key_cluster_sums + seed_means.astype(jnp.float32)) / (member_counts + 1.0)[:, :, None]).astype(jnp.bfloat16)
    key_cluster_sums, value_cluster_sums, member_counts = totals(solitary_means)
    key_centres = ((key_cluster_sums + solitary_means.astype(jnp.float32)) / (member_counts + 1.0)[:, :, None]).astype(jnp.bfloat16)
    value_centres = (value_cluster_sums / (member_counts + 1.0)[:, :, None]).astype(jnp.bfloat16)
    log_mass = jnp.log(member_counts + 1.0).astype(jnp.bfloat16)
    attended = attend(question_vectors, key_centres, value_centres, log_mass)
    return jnp.dot(attended, final_projection_matrix, preferred_element_type=jnp.float32).astype(jnp.bfloat16)
```

```python
import functools

import jax
import jax.numpy as jnp
from jax import lax
from jax.experimental import pallas as pl
from jax.experimental.pallas import tpu as pltpu
from jax.sharding import PartitionSpec as P

MESH = pl.DeviceIdType.MESH
LOG2E = 1.4426950408889634
TOKEN_TILE = 256
COLUMN_TILE = 512


def mate(j, k):
    if k == 1:
        return j + 1 - 2 * lax.rem(j, 2)
    if k == 2:
        return lax.rem(j + 2, 4)
    return 3 - j


def kernel(
    rows_of_line, heads,
    kcodes_hbm, kscale, vcodes_hbm, vscale, seed_hbm, softness, q_hbm, w_hbm,
    out_ref,
    kcodes, vcodes, qin, seed, kst, vst, kv, qbuf, c_one, kvc, csq,
    acc, cacc, sums, cnt, rs1, cr1, rs2, cr2, lmass, atts, attf, w_full,
    load_sem, loc_sem, psend, precv, rsend, rrecv,
    wr_send, wl_send, wx_send, ws_send, wf_send, wrecv,
):
    n = rows_of_line * heads
    me = lax.axis_index("ctx")
    p, j = lax.div(me, heads), lax.rem(me, heads)
    mates = [None] + [mate(j, k) for k in (1, 2, 3)]
    tokens = kcodes.shape[0]
    head_len = seed.shape[1]
    centres = seed.shape[0]
    chunk = centres // rows_of_line
    shard = w_hbm.shape[0]
    q_rows = qin.shape[0]
    q_cols = qin.shape[1] // heads
    group_len = q_cols // head_len

    def plane(k):
        return p * heads + mates[k]

    def line(k):
        return lax.rem(p + k, rows_of_line) * heads + j

    def remote(src, dst, ss, rs, dev):
        return pltpu.make_async_remote_copy(
            src_ref=src, dst_ref=dst, send_sem=ss, recv_sem=rs,
            device_id={"ctx": dev}, device_id_type=MESH,
        )

    loads = [
        pltpu.make_async_copy(kcodes_hbm, kcodes, load_sem.at[0]),
        pltpu.make_async_copy(vcodes_hbm, vcodes, load_sem.at[1]),
        pltpu.make_async_copy(q_hbm, qin, load_sem.at[2]),
        pltpu.make_async_copy(seed_hbm.at[j], seed, load_sem.at[3]),
    ]
    for item in loads:
        item.start()

    def w_rows(q, jj):
        return w_full.at[pl.ds(pl.multiple_of((q * heads + jj) * shard, shard), shard), :]

    own_w = pltpu.make_async_copy(w_hbm, w_rows(p, j), load_sem.at[4])
    own_w.start()

    barrier = pltpu.get_barrier_semaphore()
    for k in (1, 2, 3):
        pl.semaphore_signal(barrier, inc=1, device_id={"ctx": plane(k)}, device_id_type=MESH)
    for k in range(1, rows_of_line):
        pl.semaphore_signal(barrier, inc=1, device_id={"ctx": line(k)}, device_id_type=MESH)
    pl.semaphore_wait(barrier, 3 + rows_of_line - 1)

    right = jnp.minimum(p + 1, rows_of_line - 1) * heads + j
    left = jnp.maximum(p - 1, 0) * heads + j

    def w_copy(q, jj, ss, dev):
        sid = q * heads + jj
        return remote(w_rows(q, jj), w_rows(q, jj), ss, wrecv.at[sid], dev)

    def spread(q):
        w_copy(q, j, wx_send.at[q], plane(2)).start()
        w_copy(q, j, ws_send.at[q], plane(1)).start()

    def w_step(k):
        lo, hi = p - k, p + k

        @pl.when(lo >= 0)
        def _():
            q = jnp.maximum(lo, 0)
            w_copy(q, j, wr_send.at[q], right).wait_recv()

            @pl.when(p < rows_of_line - 1)
            def _():
                w_copy(q, j, wr_send.at[q], right).start()

            spread(q)

        @pl.when(hi < rows_of_line)
        def _():
            q = jnp.minimum(hi, rows_of_line - 1)
            w_copy(q, j, wl_send.at[q], left).wait_recv()

            @pl.when(p > 0)
            def _():
                w_copy(q, j, wl_send.at[q], left).start()

            spread(q)

    def x_one(q):
        w_copy(q, mates[2], wf_send.at[q], plane(1)).wait_recv()
        w_copy(q, mates[2], wf_send.at[q], plane(1)).start()

    def x_step(k):
        @pl.when(p - k >= 0)
        def _():
            x_one(jnp.maximum(p - k, 0))

        @pl.when(p + k < rows_of_line)
        def _():
            x_one(jnp.minimum(p + k, rows_of_line - 1))

    def w_stage(stage, step):
        first, last = stage * rows_of_line // 4, (stage + 1) * rows_of_line // 4
        if last - first <= 2:
            for k in range(first, last):
                if k > 0:
                    step(k)
        else:
            @pl.loop(max(first, 1), last)
            def _(k):
                step(k)

    def dequantize(codes, scale, stage, lane, base):
        block = tokens // scale.shape[0]
        for h in range(heads):
            for b in range(scale.shape[0]):
                piece = codes[b * block:(b + 1) * block, h * head_len:(h + 1) * head_len]
                stage[h, b * block:(b + 1) * block, :] = (
                    piece.astype(jnp.float32) * scale[b, h]
                ).astype(jnp.bfloat16)
        cols = pl.ds(lane * head_len, head_len)
        mine = pltpu.make_async_copy(
            stage.at[j], kv.at[pl.ds(0, tokens), cols], loc_sem.at[lane]
        )
        mine.start()
        copies = [
            remote(
                stage.at[mates[k]], kv.at[pl.ds(k * tokens, tokens), cols],
                psend.at[base + k], precv.at[base + k], plane(k),
            )
            for k in (1, 2, 3)
        ]
        for c in copies:
            c.start()
        return mine, copies

    loads[0].wait()
    k_mine, k_copies = dequantize(kcodes, kscale, kst, 0, 0)
    own_w.wait()
    for q in (p,):
        @pl.when(p < rows_of_line - 1)
        def _():
            w_copy(q, j, wr_send.at[q], right).start()

        @pl.when(p > 0)
        def _():
            w_copy(q, j, wl_send.at[q], left).start()

    loads[1].wait()
    v_mine, v_copies = dequantize(vcodes, vscale, vst, 1, 4)
    loads[2].wait()
    q_mine = pltpu.make_async_copy(
        qin.at[:, pl.ds(pl.multiple_of(j * q_cols, q_cols), q_cols)],
        qbuf.at[pl.ds(0, q_rows), :], loc_sem.at[2],
    )
    q_mine.start()
    q_copies = [
        remote(
            qin.at[:, pl.ds(pl.multiple_of(mates[k] * q_cols, q_cols), q_cols)],
            qbuf.at[pl.ds(k * q_rows, q_rows), :],
            psend.at[8 + k], precv.at[8 + k], plane(k),
        )
        for k in (1, 2, 3)
    ]
    for c in q_copies:
        c.start()
    spread(p)
    loads[3].wait()
    k_mine.wait()
    for c in k_copies:
        c.wait()

    factor = LOG2E / softness[j]

    def assign(centre, width):
        cf = centre[...].astype(jnp.float32)
        csq[...] = jnp.sum(cf * cf, axis=1, keepdims=True) * factor
        acc[:, :width] = jnp.zeros((centres, width), jnp.float32)
        cacc[...] = jnp.zeros_like(cacc)

        @pl.loop(0, heads * tokens // TOKEN_TILE)
        def _(i):
            rows = pl.ds(pl.multiple_of(i * TOKEN_TILE, TOKEN_TILE), TOKEN_TILE)
            logits = lax.dot_general(
                centre[...], kv[rows, :head_len], (((1,), (1,)), ((), ())),
                preferred_element_type=jnp.float32,
            )
            logits = logits * (2.0 * factor) - csq[...]
            e = jnp.exp2(logits - jnp.max(logits, axis=0, keepdims=True))
            weights = e * (1.0 / jnp.sum(e, axis=0, keepdims=True))
            part = weights[:, :128]
            for s in range(128, TOKEN_TILE, 128):
                part = part + weights[:, s:s + 128]
            cacc[...] += part
            acc[:, :width] += jnp.dot(
                weights.astype(jnp.bfloat16), kv[rows, :width],
                preferred_element_type=jnp.float32,
            )

        sums[:, :width] = acc[:, :width].astype(jnp.bfloat16)
        for b in range(centres // 128):
            cnt[b:b + 1, :] = jnp.sum(
                cacc[b * 128:(b + 1) * 128, :].T, axis=0, keepdims=True
            )

    def exchange_sums(width, rs, cr, base):
        copies = []
        for k in range(1, rows_of_line):
            rows = pl.ds(pl.multiple_of(lax.rem(p + k, rows_of_line) * chunk, chunk), chunk)
            copies.append(remote(
                sums.at[rows, pl.ds(0, width)], rs.at[k],
                rsend.at[base, k], rrecv.at[base, k], line(k),
            ))
            copies.append(remote(
                cnt, cr.at[k], rsend.at[base + 1, k], rrecv.at[base + 1, k], line(k),
            ))
        for c in copies:
            c.start()
        return copies

    def total_counts(cr):
        total = cnt[...]
        for k in range(1, rows_of_line):
            total = total + cr[k]
        return total + 1.0

    def columns(rows8):
        for b in range(centres // 128):
            cacc[b * 128:(b + 1) * 128, :] = jnp.broadcast_to(rows8[b:b + 1, :], (128, 128)).T

    own_rows = pl.ds(pl.multiple_of(p * chunk, chunk), chunk)

    def total_sums(rs, lanes):
        total = acc[own_rows, lanes]
        for k in range(1, rows_of_line):
            total = total + rs[k, :, lanes].astype(jnp.float32)
        return total

    def share(buf, base):
        copies = [
            remote(buf.at[own_rows, :], buf.at[own_rows, :],
                   rsend.at[base, k], rrecv.at[base, k], line(k))
            for k in range(1, rows_of_line)
        ]
        for c in copies:
            c.start()
        return copies

    def await_share(buf, base, copies):
        for k in range(1, rows_of_line):
            copies[k - 1].wait_send()
            q = lax.rem(p + rows_of_line - k, rows_of_line)
            rows = pl.ds(pl.multiple_of(q * chunk, chunk), chunk)
            remote(buf.at[rows, :], buf.at[rows, :],
                   rsend.at[base, k], rrecv.at[base, k], line(k)).wait_recv()

    assign(seed, head_len)
    copies = exchange_sums(head_len, rs1, cr1, 0)
    for c in copies:
        c.wait()
    columns(total_counts(cr1))
    c_one[own_rows, :] = (
        (total_sums(rs1, slice(0, head_len)) + seed[own_rows, :].astype(jnp.float32))
        / cacc[own_rows, :]
    ).astype(jnp.bfloat16)
    copies = share(c_one, 2)
    w_stage(0, w_step)
    w_stage(1, w_step)
    x_one(p)
    v_mine.wait()
    for c in v_copies:
        c.wait()
    await_share(c_one, 2, copies)

    assign(c_one, 2 * head_len)
    copies = exchange_sums(2 * head_len, rs2, cr2, 3)
    w_stage(0, x_step)
    for c in copies:
        c.wait()
    mass = total_counts(cr2)
    columns(mass)
    count_col = cacc[own_rows, :]
    kvc[own_rows, :head_len] = (
        (total_sums(rs2, slice(0, head_len)) + c_one[own_rows, :].astype(jnp.float32))
        / count_col
    ).astype(jnp.bfloat16)
    kvc[own_rows, head_len:] = (
        total_sums(rs2, slice(head_len, 2 * head_len)) / count_col
    ).astype(jnp.bfloat16)
    copies = share(kvc, 5)
    w_stage(2, w_step)
    w_stage(1, x_step)
    columns(jnp.log(mass).astype(jnp.bfloat16).astype(jnp.float32) * LOG2E)
    lmass[...] = cacc[:, :1]
    q_mine.wait()
    for c in q_copies:
        c.wait()
    await_share(kvc, 5, copies)

    val_t = kvc[:, head_len:].astype(jnp.float32).T.astype(jnp.bfloat16)
    scale = LOG2E / (float(head_len) ** 0.5)
    for g in range(group_len):
        cols = slice(g * head_len, (g + 1) * head_len)
        scores = lax.dot_general(
            kvc[:, :head_len], qbuf[:, cols], (((1,), (1,)), ((), ())),
            preferred_element_type=jnp.float32,
        )
        scores = scores * scale + lmass[...]
        e = jnp.exp2(scores - jnp.max(scores, axis=0, keepdims=True))
        probs = (e * (1.0 / jnp.sum(e, axis=0, keepdims=True))).astype(jnp.bfloat16)
        mixed = jnp.dot(val_t, probs, preferred_element_type=jnp.float32)
        atts[:, cols] = mixed.T.astype(jnp.bfloat16)
    a_mine = pltpu.make_async_copy(atts.at[pl.ds(0, q_rows), :], attf.at[j], loc_sem.at[3])
    a_mine.start()
    a_copies = [
        remote(
            atts.at[pl.ds(k * q_rows, q_rows), :], attf.at[j],
            psend.at[12 + k], precv.at[12 + k], plane(k),
        )
        for k in (1, 2, 3)
    ]
    for c in a_copies:
        c.start()
    w_stage(3, w_step)
    w_stage(2, x_step)
    w_stage(3, x_step)
    a_mine.wait()
    for k in (1, 2, 3):
        a_copies[k - 1].wait_send()
        remote(
            atts.at[pl.ds(0, q_rows), :], attf.at[mates[k]],
            psend.at[12 + k], precv.at[12 + k], plane(k),
        ).wait_recv()

    @pl.loop(0, rows_of_line)
    def _(q):
        w_copy(q, mates[1], ws_send.at[q], plane(1)).wait_recv()
        w_copy(q, mates[3], ws_send.at[q], plane(1)).wait_recv()
        w_copy(q, j, ws_send.at[q], plane(1)).wait_send()
        w_copy(q, j, wx_send.at[q], plane(2)).wait_send()
        w_copy(q, mates[2], wf_send.at[q], plane(1)).wait_send()

        @pl.when((q <= p) & (p < rows_of_line - 1))
        def _():
            w_copy(q, j, wr_send.at[q], right).wait_send()

        @pl.when((q >= p) & (p > 0))
        def _():
            w_copy(q, j, wl_send.at[q], left).wait_send()

    left_side = jnp.concatenate([attf[h] for h in range(heads)], axis=1)

    @pl.loop(0, w_full.shape[1] // COLUMN_TILE)
    def _(i):
        cols = pl.ds(pl.multiple_of(i * COLUMN_TILE, COLUMN_TILE), COLUMN_TILE)
        out_ref[:, cols] = jnp.dot(
            left_side, w_full[:, cols], preferred_element_type=jnp.float32
        ).astype(out_ref.dtype)


def per_device(n, kcodes, kscale, vcodes, vscale, seed, softness, questions, weight):
    heads, centres, head_len = seed.shape
    line = n // heads
    tokens = kcodes.shape[0]
    q_rows, q_width = questions.shape
    depth, width = weight.shape
    chunk = centres // line
    bf16, f32 = jnp.bfloat16, jnp.float32
    vm = pltpu.VMEM
    dma = pltpu.SemaphoreType.DMA
    anywhere = pl.BlockSpec(memory_space=pl.ANY)
    scalars = pl.BlockSpec(memory_space=pltpu.SMEM)
    q_cols = q_width // heads
    return pl.pallas_call(
        functools.partial(kernel, line, heads),
        out_shape=jax.ShapeDtypeStruct((q_rows, width), bf16),
        in_specs=[anywhere, scalars, anywhere, scalars, anywhere, scalars, anywhere, anywhere],
        out_specs=pl.BlockSpec(memory_space=pltpu.VMEM),
        scratch_shapes=[
            vm(kcodes.shape, kcodes.dtype),
            vm(vcodes.shape, vcodes.dtype),
            vm(questions.shape, bf16),
            vm((centres, head_len), bf16),
            vm((heads, tokens, head_len), bf16),
            vm((heads, tokens, head_len), bf16),
            vm((heads * tokens, 2 * head_len), bf16),
            vm((heads * q_rows, q_cols), bf16),
            vm((centres, head_len), bf16),
            vm((centres, 2 * head_len), bf16),
            vm((centres, 1), f32),
            vm((centres, 2 * head_len), f32),
            vm((centres, 128), f32),
            vm((centres, 2 * head_len), bf16),
            vm((centres // 128, 128), f32),
            vm((line, chunk, head_len), bf16),
            vm((line, centres // 128, 128), f32),
            vm((line, chunk, 2 * head_len), bf16),
            vm((line, centres // 128, 128), f32),
            vm((centres, 1), f32),
            vm((heads * q_rows, q_cols), bf16),
            vm((heads, q_rows, q_cols), bf16),
            vm((n * depth, width), bf16),
            dma((5,)),
            dma((4,)),
            dma((16,)),
            dma((16,)),
            dma((6, line)),
            dma((6, line)),
            dma((line,)),
            dma((line,)),
            dma((line,)),
            dma((line,)),
            dma((line,)),
            dma((n,)),
        ],
        compiler_params=pltpu.CompilerParams(
            collective_id=0, has_side_effects=True, vmem_limit_bytes=60 * 1024 * 1024
        ),
    )(kcodes, kscale, vcodes, vscale, seed, softness, questions, weight)


def solution(mesh):
    in_specs = (
        P(("groups", "ctx"), None),
        P(("groups", "ctx"), None),
        P(("groups", "ctx"), None),
        P(("groups", "ctx"), None),
        P("groups", None, None),
        P("groups"),
        P(("groups", "ctx"), None),
        P("ctx", None),
    )
    out_specs = P(("groups", "ctx"), None)
    return jax.shard_map(
        functools.partial(per_device, mesh.shape["ctx"]),
        mesh=mesh, in_specs=in_specs, out_specs=out_specs, check_vma=False,
    )
```

```python
import functools

import jax
import jax.numpy as jnp
from jax import lax
from jax.experimental import pallas as pl
from jax.experimental.pallas import tpu as pltpu
from jax.sharding import PartitionSpec as P

MESH = pl.DeviceIdType.MESH
LOG2E = 1.4426950408889634
TOKEN_TILE = 256
HOOKS = (4, 0)
COLUMN_TILES = 4


def mate(j, k):
    if k == 1:
        return j + 1 - 2 * lax.rem(j, 2)
    if k == 2:
        return lax.rem(j + 2, 4)
    return 3 - j


def kernel(
    rows_of_line, heads, halves,
    kcodes_hbm, kscale, vcodes_hbm, vscale, seed_hbm, softness, q_hbm, w_hbm,
    out_ref,
    kcodes, vcodes, qin, seed, kst, vst, kv, qbuf, c_one, kvc, csq,
    acc, cacc, sums, cnt, rs1, cr1, rs2, cr2, lmass, atts, xin, w_line, yf, sib_out, sib_in, x_out, x_in,
    load_sem, loc_sem, psend, precv, rsend, rrecv,
    wr_send, wl_send, wy_send, wrecv, wyrecv, tsend, trecv,
):
    n = rows_of_line * heads
    me = lax.axis_index("ctx")
    p, j = lax.div(me, heads), lax.rem(me, heads)
    mates = [None] + [mate(j, k) for k in (1, 2, 3)]
    tokens = kcodes.shape[0]
    head_len = seed.shape[1]
    centres = seed.shape[0]
    chunk = centres // rows_of_line
    shard = w_hbm.shape[0]
    q_rows = qin.shape[0]
    q_cols = qin.shape[1] // heads
    group_len = q_cols // head_len

    def plane(k):
        return p * heads + mates[k]

    def line(k):
        return lax.rem(p + k, rows_of_line) * heads + j

    def remote(src, dst, ss, rs, dev):
        return pltpu.make_async_remote_copy(
            src_ref=src, dst_ref=dst, send_sem=ss, recv_sem=rs,
            device_id={"ctx": dev}, device_id_type=MESH,
        )

    loads = [
        pltpu.make_async_copy(kcodes_hbm, kcodes, load_sem.at[0]),
        pltpu.make_async_copy(vcodes_hbm, vcodes, load_sem.at[1]),
        pltpu.make_async_copy(q_hbm, qin, load_sem.at[2]),
        pltpu.make_async_copy(seed_hbm.at[j], seed, load_sem.at[3]),
    ]
    for item in loads:
        item.start()

    half = w_hbm.shape[1] // halves
    group = lax.axis_index("groups")
    ours = pl.multiple_of((group if halves == 2 else 0) * half, half)
    w_cols = pl.ds(ours, half)

    def w_part(q):
        return w_line.at[pl.ds(pl.multiple_of(q * shard, shard), shard), w_cols]

    own_w = pltpu.make_async_copy(
        w_hbm, w_line.at[pl.ds(pl.multiple_of(p * shard, shard), shard), :], load_sem.at[4]
    )
    own_w.start()

    barrier = pltpu.get_barrier_semaphore()
    for k in (1, 2, 3):
        pl.semaphore_signal(barrier, inc=1, device_id={"ctx": plane(k)}, device_id_type=MESH)
    for k in range(1, rows_of_line):
        pl.semaphore_signal(barrier, inc=1, device_id={"ctx": line(k)}, device_id_type=MESH)
    if halves == 2:
        pl.semaphore_signal(
            barrier, inc=1, device_id={"groups": 1 - group, "ctx": me}, device_id_type=MESH
        )
    pl.semaphore_wait(barrier, 3 + rows_of_line - 1 + halves - 1)

    right = jnp.minimum(p + 1, rows_of_line - 1) * heads + j
    left = jnp.maximum(p - 1, 0) * heads + j

    def w_copy(q, ss, dev):
        return remote(w_part(q), w_part(q), ss, wrecv.at[q], dev)

    def twin(q):
        return pltpu.make_async_remote_copy(
            src_ref=w_part(q), dst_ref=w_part(q), send_sem=wy_send.at[q],
            recv_sem=wyrecv.at[q], device_id={"groups": 1 - group, "ctx": me},
            device_id_type=MESH,
        )

    def twin_arrival(q):
        there = pl.ds(pl.multiple_of((1 - group) * half, half), half)
        part = w_line.at[pl.ds(pl.multiple_of(q * shard, shard), shard), there]
        return pltpu.make_async_remote_copy(
            src_ref=part, dst_ref=part, send_sem=wy_send.at[q],
            recv_sem=wyrecv.at[q], device_id={"groups": 1 - group, "ctx": me},
            device_id_type=MESH,
        )

    def w_step(k):
        lo, hi = p - k, p + k

        @pl.when(lo >= 0)
        def _():
            q = jnp.maximum(lo, 0)
            w_copy(q, wr_send.at[q], right).wait_recv()

            @pl.when(p < rows_of_line - 1)
            def _():
                w_copy(q, wr_send.at[q], right).start()

            if halves == 2:
                twin(q).start()

        @pl.when(hi < rows_of_line)
        def _():
            q = jnp.minimum(hi, rows_of_line - 1)
            w_copy(q, wl_send.at[q], left).wait_recv()

            @pl.when(p > 0)
            def _():
                w_copy(q, wl_send.at[q], left).start()

            if halves == 2:
                twin(q).start()

    def w_stage(stage, step):
        first, last = stage * rows_of_line // 4, (stage + 1) * rows_of_line // 4
        if last - first <= 2:
            for k in range(first, last):
                if k > 0:
                    step(k)
        else:
            @pl.loop(max(first, 1), last)
            def _(k):
                step(k)

    def dequantize(codes, scale, stage, lane, base):
        block = tokens // scale.shape[0]
        for h in range(heads):
            for b in range(scale.shape[0]):
                piece = codes[b * block:(b + 1) * block, h * head_len:(h + 1) * head_len]
                stage[h, b * block:(b + 1) * block, :] = (
                    piece.astype(jnp.float32) * scale[b, h]
                ).astype(jnp.bfloat16)
        cols = pl.ds(lane * head_len, head_len)
        mine = pltpu.make_async_copy(
            stage.at[j], kv.at[pl.ds(0, tokens), cols], loc_sem.at[lane]
        )
        mine.start()
        copies = [
            remote(
                stage.at[mates[k]], kv.at[pl.ds(k * tokens, tokens), cols],
                psend.at[base + k], precv.at[base + k], plane(k),
            )
            for k in (1, 2, 3)
        ]
        for c in copies:
            c.start()
        return mine, copies

    loads[0].wait()
    k_mine, k_copies = dequantize(kcodes, kscale, kst, 0, 0)
    own_w.wait()

    @pl.when(p < rows_of_line - 1)
    def _():
        w_copy(p, wr_send.at[p], right).start()

    @pl.when(p > 0)
    def _():
        w_copy(p, wl_send.at[p], left).start()

    loads[1].wait()
    v_mine, v_copies = dequantize(vcodes, vscale, vst, 1, 4)
    loads[2].wait()
    own_queries = pl.ds(pl.multiple_of(j * q_rows, q_rows), q_rows)
    q_mine = pltpu.make_async_copy(
        qin.at[:, pl.ds(pl.multiple_of(j * q_cols, q_cols), q_cols)],
        qbuf.at[own_queries, :], loc_sem.at[2],
    )
    q_mine.start()
    q_copies = [
        remote(
            qin.at[:, pl.ds(pl.multiple_of(mates[k] * q_cols, q_cols), q_cols)],
            qbuf.at[own_queries, :],
            psend.at[8 + k], precv.at[8 + k], plane(k),
        )
        for k in (1, 2, 3)
    ]
    for c in q_copies:
        c.start()
    loads[3].wait()
    k_mine.wait()
    for c in k_copies:
        c.wait()

    factor = LOG2E / softness[j]

    def assign(centre, width, hook_at, hook):
        cf = centre[...].astype(jnp.float32)
        csq[...] = jnp.sum(cf * cf, axis=1, keepdims=True) * factor
        acc[:, :width] = jnp.zeros((centres, width), jnp.float32)
        cacc[...] = jnp.zeros_like(cacc)

        def tile(i):
            rows = pl.ds(pl.multiple_of(i * TOKEN_TILE, TOKEN_TILE), TOKEN_TILE)
            logits = lax.dot_general(
                centre[...], kv[rows, :head_len], (((1,), (1,)), ((), ())),
                preferred_element_type=jnp.float32,
            )
            logits = logits * (2.0 * factor) - csq[...]
            e = jnp.exp2(logits - jnp.max(logits, axis=0, keepdims=True))
            weights = e * (1.0 / jnp.sum(e, axis=0, keepdims=True))
            part = weights[:, :128]
            for s in range(128, TOKEN_TILE, 128):
                part = part + weights[:, s:s + 128]
            cacc[...] += part
            acc[:, :width] += jnp.dot(
                weights.astype(jnp.bfloat16), kv[rows, :width],
                preferred_element_type=jnp.float32,
            )

        tiles = heads * tokens // TOKEN_TILE
        pl.loop(0, hook_at)(tile)
        hook()
        pl.loop(hook_at, tiles)(tile)
        sums[:, :width] = acc[:, :width].astype(jnp.bfloat16)
        for b in range(centres // 128):
            cnt[b:b + 1, :] = jnp.sum(
                cacc[b * 128:(b + 1) * 128, :].T, axis=0, keepdims=True
            )

    def exchange_sums(width, rs, cr, base):
        copies = []
        for k in range(1, rows_of_line):
            rows = pl.ds(pl.multiple_of(lax.rem(p + k, rows_of_line) * chunk, chunk), chunk)
            copies.append(remote(
                sums.at[rows, pl.ds(0, width)], rs.at[k],
                rsend.at[base, k], rrecv.at[base, k], line(k),
            ))
            copies.append(remote(
                cnt, cr.at[k], rsend.at[base + 1, k], rrecv.at[base + 1, k], line(k),
            ))
        for c in copies:
            c.start()
        return copies

    def total_counts(cr):
        total = cnt[...]
        for k in range(1, rows_of_line):
            total = total + cr[k]
        return total + 1.0

    def columns(rows8):
        for b in range(centres // 128):
            cacc[b * 128:(b + 1) * 128, :] = jnp.broadcast_to(rows8[b:b + 1, :], (128, 128)).T

    own_rows = pl.ds(pl.multiple_of(p * chunk, chunk), chunk)

    def total_sums(rs, lanes):
        total = acc[own_rows, lanes]
        for k in range(1, rows_of_line):
            total = total + rs[k, :, lanes].astype(jnp.float32)
        return total

    def share(buf, base):
        copies = [
            remote(buf.at[own_rows, :], buf.at[own_rows, :],
                   rsend.at[base, k], rrecv.at[base, k], line(k))
            for k in range(1, rows_of_line)
        ]
        for c in copies:
            c.start()
        return copies

    def await_share(buf, base, copies):
        for k in range(1, rows_of_line):
            copies[k - 1].wait_send()
            q = lax.rem(p + rows_of_line - k, rows_of_line)
            rows = pl.ds(pl.multiple_of(q * chunk, chunk), chunk)
            remote(buf.at[rows, :], buf.at[rows, :],
                   rsend.at[base, k], rrecv.at[base, k], line(k)).wait_recv()

    assign(seed, head_len, HOOKS[0], lambda: (w_stage(0, w_step), w_stage(1, w_step)))
    copies = exchange_sums(head_len, rs1, cr1, 0)
    for c in copies:
        c.wait()
    columns(total_counts(cr1))
    c_one[own_rows, :] = (
        (total_sums(rs1, slice(0, head_len)) + seed[own_rows, :].astype(jnp.float32))
        / cacc[own_rows, :]
    ).astype(jnp.bfloat16)
    copies = share(c_one, 2)
    v_mine.wait()
    for c in v_copies:
        c.wait()
    await_share(c_one, 2, copies)

    assign(c_one, 2 * head_len, HOOKS[1], lambda: w_stage(2, w_step))
    copies = exchange_sums(2 * head_len, rs2, cr2, 3)
    for c in copies:
        c.wait()
    mass = total_counts(cr2)
    columns(mass)
    count_col = cacc[own_rows, :]
    kvc[own_rows, :head_len] = (
        (total_sums(rs2, slice(0, head_len)) + c_one[own_rows, :].astype(jnp.float32))
        / count_col
    ).astype(jnp.bfloat16)
    kvc[own_rows, head_len:] = (
        total_sums(rs2, slice(head_len, 2 * head_len)) / count_col
    ).astype(jnp.bfloat16)
    copies = share(kvc, 5)
    columns(jnp.log(mass).astype(jnp.bfloat16).astype(jnp.float32) * LOG2E)
    lmass[...] = cacc[:, :1]
    q_mine.wait()
    for c in q_copies:
        c.wait()
    await_share(kvc, 5, copies)

    w_stage(3, w_step)
    val_t = kvc[:, head_len:].astype(jnp.float32).T.astype(jnp.bfloat16)
    scale = LOG2E / (float(head_len) ** 0.5)
    for g in range(group_len):
        cols = slice(g * head_len, (g + 1) * head_len)
        scores = lax.dot_general(
            kvc[:, :head_len], qbuf[:, cols], (((1,), (1,)), ((), ())),
            preferred_element_type=jnp.float32,
        )
        scores = scores * scale + lmass[...]
        e = jnp.exp2(scores - jnp.max(scores, axis=0, keepdims=True))
        probs = (e * (1.0 / jnp.sum(e, axis=0, keepdims=True))).astype(jnp.bfloat16)
        mixed = jnp.dot(val_t, probs, preferred_element_type=jnp.float32)
        atts[:, cols] = mixed.T.astype(jnp.bfloat16)
    piece = q_cols // heads
    if shard != piece:
        src = lax.broadcasted_iota(jnp.int32, (q_cols, q_cols), 0)
        dst = lax.broadcasted_iota(jnp.int32, (q_cols, q_cols), 1)
        block = src // shard
        target = (block % heads) * piece + (block // heads) * shard + src % shard
        order = jnp.where(dst == target, 1.0, 0.0).astype(jnp.bfloat16)
        atts[...] = jnp.dot(
            atts[...], order, preferred_element_type=jnp.float32
        ).astype(jnp.bfloat16)

    def member(m):
        return pl.ds(pl.multiple_of(m * piece, piece), piece)

    a_mine = pltpu.make_async_copy(
        atts.at[:, member(j)], xin.at[:, member(j)], loc_sem.at[3]
    )
    a_mine.start()
    a_copies = [
        remote(
            atts.at[:, member(mates[k])], xin.at[:, member(j)],
            psend.at[12 + k], precv.at[12 + k], plane(k),
        )
        for k in (1, 2, 3)
    ]
    for c in a_copies:
        c.start()

    @pl.loop(0, rows_of_line)
    def _(q):
        @pl.when((q <= p) & (p < rows_of_line - 1))
        def _():
            w_copy(q, wr_send.at[q], right).wait_send()

        @pl.when((q >= p) & (p > 0))
        def _():
            w_copy(q, wl_send.at[q], left).wait_send()

        if halves == 2:
            @pl.when(q != p)
            def _():
                twin_arrival(q).wait_recv()
                twin(q).wait_send()

    a_mine.wait()
    for k in (1, 2, 3):
        a_copies[k - 1].wait_send()
        remote(
            atts.at[:, member(mates[k])], xin.at[:, member(mates[k])],
            psend.at[12 + k], precv.at[12 + k], plane(k),
        ).wait_recv()

    width = w_line.shape[1] // COLUMN_TILES

    def block_of(m):
        return pl.ds(pl.multiple_of(m * q_rows, q_rows), q_rows)

    def to_sibling(t):
        return remote(
            sib_out.at[t], sib_in.at[t], tsend.at[0, t], trecv.at[0, t], plane(1)
        )

    def to_chip(t):
        return remote(x_out.at[t], x_in.at[t], tsend.at[1, t], trecv.at[1, t], plane(2))

    def pass_on(t):
        cols = slice(t * width, (t + 1) * width)
        to_sibling(t).wait_recv()
        x_out[t] = (
            yf[block_of(mates[2]), cols] + sib_in[t, q_rows:, :].astype(jnp.float32)
        ).astype(jnp.bfloat16)
        to_chip(t).start()

    for t in range(COLUMN_TILES):
        cols = slice(t * width, (t + 1) * width)
        yf[:, cols] = jnp.dot(xin[...], w_line[:, cols], preferred_element_type=jnp.float32)
        sib_out[t, :q_rows, :] = yf[block_of(mates[1]), cols].astype(jnp.bfloat16)
        sib_out[t, q_rows:, :] = yf[block_of(mates[3]), cols].astype(jnp.bfloat16)
        to_sibling(t).start()
        if t > 0:
            pass_on(t - 1)
    pass_on(COLUMN_TILES - 1)
    for t in range(COLUMN_TILES):
        cols = slice(t * width, (t + 1) * width)
        to_sibling(t).wait_send()
        to_chip(t).wait()
        out_ref[:, cols] = (
            yf[block_of(j), cols]
            + sib_in[t, :q_rows, :].astype(jnp.float32)
            + x_in[t].astype(jnp.float32)
        ).astype(out_ref.dtype)


def per_device(n, halves, kcodes, kscale, vcodes, vscale, seed, softness, questions, weight):
    heads, centres, head_len = seed.shape
    line = n // heads
    tokens = kcodes.shape[0]
    q_rows, q_width = questions.shape
    depth, width = weight.shape
    chunk = centres // line
    bf16, f32 = jnp.bfloat16, jnp.float32
    vm = pltpu.VMEM
    dma = pltpu.SemaphoreType.DMA
    anywhere = pl.BlockSpec(memory_space=pl.ANY)
    scalars = pl.BlockSpec(memory_space=pltpu.SMEM)
    q_cols = q_width // heads
    return pl.pallas_call(
        functools.partial(kernel, line, heads, halves),
        out_shape=jax.ShapeDtypeStruct((q_rows, width), bf16),
        in_specs=[anywhere, scalars, anywhere, scalars, anywhere, scalars, anywhere, anywhere],
        out_specs=pl.BlockSpec(memory_space=pltpu.VMEM),
        scratch_shapes=[
            vm(kcodes.shape, kcodes.dtype),
            vm(vcodes.shape, vcodes.dtype),
            vm(questions.shape, bf16),
            vm((centres, head_len), bf16),
            vm((heads, tokens, head_len), bf16),
            vm((heads, tokens, head_len), bf16),
            vm((heads * tokens, 2 * head_len), bf16),
            vm((heads * q_rows, q_cols), bf16),
            vm((centres, head_len), bf16),
            vm((centres, 2 * head_len), bf16),
            vm((centres, 1), f32),
            vm((centres, 2 * head_len), f32),
            vm((centres, 128), f32),
            vm((centres, 2 * head_len), bf16),
            vm((centres // 128, 128), f32),
            vm((line, chunk, head_len), bf16),
            vm((line, centres // 128, 128), f32),
            vm((line, chunk, 2 * head_len), bf16),
            vm((line, centres // 128, 128), f32),
            vm((centres, 1), f32),
            vm((heads * q_rows, q_cols), bf16),
            vm((heads * q_rows, q_cols), bf16),
            vm((line * depth, width), bf16),
            vm((heads * q_rows, width), f32),
            vm((COLUMN_TILES, 2 * q_rows, width // COLUMN_TILES), bf16),
            vm((COLUMN_TILES, 2 * q_rows, width // COLUMN_TILES), bf16),
            vm((COLUMN_TILES, q_rows, width // COLUMN_TILES), bf16),
            vm((COLUMN_TILES, q_rows, width // COLUMN_TILES), bf16),
            dma((5,)),
            dma((4,)),
            dma((16,)),
            dma((16,)),
            dma((6, line)),
            dma((6, line)),
            dma((line,)),
            dma((line,)),
            dma((line,)),
            dma((line,)),
            dma((line,)),
            dma((2, COLUMN_TILES)),
            dma((2, COLUMN_TILES)),
        ],
        compiler_params=pltpu.CompilerParams(
            collective_id=0, has_side_effects=True, vmem_limit_bytes=60 * 1024 * 1024
        ),
    )(kcodes, kscale, vcodes, vscale, seed, softness, questions, weight)


def solution(mesh):
    in_specs = (
        P(("groups", "ctx"), None),
        P(("groups", "ctx"), None),
        P(("groups", "ctx"), None),
        P(("groups", "ctx"), None),
        P("groups", None, None),
        P("groups"),
        P(("groups", "ctx"), None),
        P("ctx", None),
    )
    out_specs = P(("groups", "ctx"), None)
    return jax.shard_map(
        functools.partial(
            per_device, mesh.shape["ctx"], 2 if mesh.shape["groups"] == 2 else 1
        ),
        mesh=mesh, in_specs=in_specs, out_specs=out_specs, check_vma=False,
    )
```

```python
import functools

import jax
import jax.numpy as jnp
from jax import lax
from jax.experimental import pallas as pl
from jax.experimental.pallas import tpu as pltpu
from jax.sharding import PartitionSpec as P

MESH = pl.DeviceIdType.MESH
LOG2E = 1.4426950408889634
TOKEN_TILE = 256
HOOKS = (4, 0)

COLUMN_TILES = 4


def mate(j, k):
    if k == 1:
        return j + 1 - 2 * lax.rem(j, 2)
    if k == 2:
        return lax.rem(j + 2, 4)
    return 3 - j


def kernel(
    rows_of_line, heads, halves,
    kcodes_hbm, kscale, vcodes_hbm, vscale, seed_hbm, softness, q_hbm, w_hbm,
    out_ref,
    kcodes, vcodes, qin, seed, kst, vst, kv, qbuf, c_one, kvc, csq,
    acc, cacc, sums, cnt, rs1, cr1, rs2, cr2, lmass, atts, xin, probs, w_line, yf, sib_out, sib_in, x_out, x_in,
    load_sem, loc_sem, psend, precv, rsend, rrecv,
    wr_send, wl_send, wy_send, wrecv, wyrecv, tsend, trecv,
):
    n = rows_of_line * heads
    me = lax.axis_index("ctx")
    p, j = lax.div(me, heads), lax.rem(me, heads)
    mates = [None] + [mate(j, k) for k in (1, 2, 3)]
    tokens = kcodes.shape[0]
    head_len = seed.shape[1]
    centres = seed.shape[0]
    chunk = centres // rows_of_line
    shard = w_hbm.shape[0]
    q_rows = qin.shape[0]
    q_cols = qin.shape[1] // heads
    group_len = q_cols // head_len

    def plane(k):
        return p * heads + mates[k]

    def line(k):
        return lax.rem(p + k, rows_of_line) * heads + j

    def remote(src, dst, ss, rs, dev):
        return pltpu.make_async_remote_copy(
            src_ref=src, dst_ref=dst, send_sem=ss, recv_sem=rs,
            device_id={"ctx": dev}, device_id_type=MESH,
        )

    loads = [
        pltpu.make_async_copy(kcodes_hbm, kcodes, load_sem.at[0]),
        pltpu.make_async_copy(vcodes_hbm, vcodes, load_sem.at[1]),
        pltpu.make_async_copy(q_hbm, qin, load_sem.at[2]),
        pltpu.make_async_copy(seed_hbm.at[j], seed, load_sem.at[3]),
    ]
    for item in loads:
        item.start()

    half = w_hbm.shape[1] // halves
    group = lax.axis_index("groups")
    ours = pl.multiple_of((group if halves == 2 else 0) * half, half)
    w_cols = pl.ds(ours, half)

    def w_part(q):
        return w_line.at[pl.ds(pl.multiple_of(q * shard, shard), shard), w_cols]

    own_w = pltpu.make_async_copy(
        w_hbm, w_line.at[pl.ds(pl.multiple_of(p * shard, shard), shard), :], load_sem.at[4]
    )
    own_w.start()

    barrier = pltpu.get_barrier_semaphore()
    for k in (1, 2, 3):
        pl.semaphore_signal(barrier, inc=1, device_id={"ctx": plane(k)}, device_id_type=MESH)
    for k in range(1, rows_of_line):
        pl.semaphore_signal(barrier, inc=1, device_id={"ctx": line(k)}, device_id_type=MESH)
    if halves == 2:
        pl.semaphore_signal(
            barrier, inc=1, device_id={"groups": 1 - group, "ctx": me}, device_id_type=MESH
        )
    pl.semaphore_wait(barrier, 3 + rows_of_line - 1 + halves - 1)

    right = jnp.minimum(p + 1, rows_of_line - 1) * heads + j
    left = jnp.maximum(p - 1, 0) * heads + j

    def w_copy(q, ss, dev):
        return remote(w_part(q), w_part(q), ss, wrecv.at[q], dev)

    def twin(q):
        return pltpu.make_async_remote_copy(
            src_ref=w_part(q), dst_ref=w_part(q), send_sem=wy_send.at[q],
            recv_sem=wyrecv.at[q], device_id={"groups": 1 - group, "ctx": me},
            device_id_type=MESH,
        )

    def twin_arrival(q):
        there = pl.ds(pl.multiple_of((1 - group) * half, half), half)
        part = w_line.at[pl.ds(pl.multiple_of(q * shard, shard), shard), there]
        return pltpu.make_async_remote_copy(
            src_ref=part, dst_ref=part, send_sem=wy_send.at[q],
            recv_sem=wyrecv.at[q], device_id={"groups": 1 - group, "ctx": me},
            device_id_type=MESH,
        )

    def w_step(k):
        lo, hi = p - k, p + k

        @pl.when(lo >= 0)
        def _():
            q = jnp.maximum(lo, 0)
            w_copy(q, wr_send.at[q], right).wait_recv()

            @pl.when(p < rows_of_line - 1)
            def _():
                w_copy(q, wr_send.at[q], right).start()

            if halves == 2:
                twin(q).start()

        @pl.when(hi < rows_of_line)
        def _():
            q = jnp.minimum(hi, rows_of_line - 1)
            w_copy(q, wl_send.at[q], left).wait_recv()

            @pl.when(p > 0)
            def _():
                w_copy(q, wl_send.at[q], left).start()

            if halves == 2:
                twin(q).start()

    def w_stage(stage, step):
        first, last = stage * rows_of_line // 4, (stage + 1) * rows_of_line // 4
        if last - first <= 2:
            for k in range(first, last):
                if k > 0:
                    step(k)
        else:
            @pl.loop(max(first, 1), last)
            def _(k):
                step(k)

    def dequantize(codes, scale, stage, lane, base):
        block = tokens // scale.shape[0]
        for h in range(heads):
            for b in range(scale.shape[0]):
                piece = codes[b * block:(b + 1) * block, h * head_len:(h + 1) * head_len]
                stage[h, b * block:(b + 1) * block, :] = (
                    piece.astype(jnp.float32) * scale[b, h]
                ).astype(jnp.bfloat16)
        cols = pl.ds(lane * head_len, head_len)
        mine = pltpu.make_async_copy(
            stage.at[j], kv.at[pl.ds(0, tokens), cols], loc_sem.at[lane]
        )
        mine.start()
        copies = [
            remote(
                stage.at[mates[k]], kv.at[pl.ds(k * tokens, tokens), cols],
                psend.at[base + k], precv.at[base + k], plane(k),
            )
            for k in (1, 2, 3)
        ]
        for c in copies:
            c.start()
        return mine, copies

    loads[0].wait()
    k_mine, k_copies = dequantize(kcodes, kscale, kst, 0, 0)
    own_w.wait()

    @pl.when(p < rows_of_line - 1)
    def _():
        w_copy(p, wr_send.at[p], right).start()

    @pl.when(p > 0)
    def _():
        w_copy(p, wl_send.at[p], left).start()

    loads[1].wait()
    v_mine, v_copies = dequantize(vcodes, vscale, vst, 1, 4)
    loads[2].wait()
    own_queries = pl.ds(pl.multiple_of(j * q_rows, q_rows), q_rows)
    q_mine = pltpu.make_async_copy(
        qin.at[:, pl.ds(pl.multiple_of(j * q_cols, q_cols), q_cols)],
        qbuf.at[own_queries, :], loc_sem.at[2],
    )
    q_mine.start()
    q_copies = [
        remote(
            qin.at[:, pl.ds(pl.multiple_of(mates[k] * q_cols, q_cols), q_cols)],
            qbuf.at[own_queries, :],
            psend.at[8 + k], precv.at[8 + k], plane(k),
        )
        for k in (1, 2, 3)
    ]
    for c in q_copies:
        c.start()
    loads[3].wait()

    factor = LOG2E / softness[j]

    def assign(centre, width, hooks):
        cf = centre[...].astype(jnp.float32)
        csq[...] = jnp.sum(cf * cf, axis=1, keepdims=True) * factor
        acc[:, :width] = jnp.zeros((centres, width), jnp.float32)
        cacc[...] = jnp.zeros_like(cacc)

        def tile(i):
            rows = pl.ds(pl.multiple_of(i * TOKEN_TILE, TOKEN_TILE), TOKEN_TILE)
            logits = lax.dot_general(
                centre[...], kv[rows, :head_len], (((1,), (1,)), ((), ())),
                preferred_element_type=jnp.float32,
            )
            logits = logits * (2.0 * factor) - csq[...]
            e = jnp.exp2(logits - jnp.max(logits, axis=0, keepdims=True))
            weights = e * (1.0 / jnp.sum(e, axis=0, keepdims=True))
            part = weights[:, :128]
            for s in range(128, TOKEN_TILE, 128):
                part = part + weights[:, s:s + 128]
            cacc[...] += part
            acc[:, :width] += jnp.dot(
                weights.astype(jnp.bfloat16), kv[rows, :width],
                preferred_element_type=jnp.float32,
            )

        tiles = heads * tokens // TOKEN_TILE
        stops = sorted({0, tiles, *(at for at, _ in hooks)})
        for first, last in zip(stops, stops[1:]):
            for at, hook in hooks:
                if at == first:
                    hook()
            pl.loop(first, last)(tile)
        sums[:, :width] = acc[:, :width].astype(jnp.bfloat16)
        for b in range(centres // 128):
            cnt[b:b + 1, :] = jnp.sum(
                cacc[b * 128:(b + 1) * 128, :].T, axis=0, keepdims=True
            )

    keys, vals = pl.ds(0, head_len), pl.ds(head_len, head_len)

    def exchange_sums(lanes, rs, base):
        copies = []
        for k in range(1, rows_of_line):
            rows = pl.ds(pl.multiple_of(lax.rem(p + k, rows_of_line) * chunk, chunk), chunk)
            copies.append(remote(
                sums.at[rows, lanes], rs.at[k, :, lanes],
                rsend.at[base, k], rrecv.at[base, k], line(k),
            ))
        for c in copies:
            c.start()
        return copies

    def exchange_counts(cr, base):
        copies = [
            remote(cnt, cr.at[k], rsend.at[base, k], rrecv.at[base, k], line(k))
            for k in range(1, rows_of_line)
        ]
        for c in copies:
            c.start()
        return copies

    def total_counts(cr):
        total = cnt[...]
        for k in range(1, rows_of_line):
            total = total + cr[k]
        return total + 1.0

    def columns(rows8):
        for b in range(centres // 128):
            cacc[b * 128:(b + 1) * 128, :] = jnp.broadcast_to(rows8[b:b + 1, :], (128, 128)).T

    own_rows = pl.ds(pl.multiple_of(p * chunk, chunk), chunk)

    def total_sums(rs, lanes):
        total = acc[own_rows, lanes]
        for k in range(1, rows_of_line):
            total = total + rs[k, :, lanes].astype(jnp.float32)
        return total

    def share(buf, lanes, base):
        copies = [
            remote(buf.at[own_rows, lanes], buf.at[own_rows, lanes],
                   rsend.at[base, k], rrecv.at[base, k], line(k))
            for k in range(1, rows_of_line)
        ]
        for c in copies:
            c.start()
        return copies

    def await_share(buf, lanes, base, copies):
        for k in range(1, rows_of_line):
            copies[k - 1].wait_send()
            q = lax.rem(p + rows_of_line - k, rows_of_line)
            rows = pl.ds(pl.multiple_of(q * chunk, chunk), chunk)
            remote(buf.at[rows, lanes], buf.at[rows, lanes],
                   rsend.at[base, k], rrecv.at[base, k], line(k)).wait_recv()

    slot = tokens // TOKEN_TILE
    assign(seed, head_len, [
        (0, k_mine.wait), (slot, k_copies[0].wait),
        (2 * slot, k_copies[1].wait), (3 * slot, k_copies[2].wait),
        (HOOKS[0], lambda: (w_stage(0, w_step), w_stage(1, w_step))),
    ])
    copies = exchange_counts(cr1, 1) + exchange_sums(keys, rs1, 0)
    for c in copies:
        c.wait()
    columns(total_counts(cr1))
    c_one[own_rows, :] = (
        (total_sums(rs1, slice(0, head_len)) + seed[own_rows, :].astype(jnp.float32))
        / cacc[own_rows, :]
    ).astype(jnp.bfloat16)
    copies = share(c_one, keys, 2)
    v_mine.wait()
    for c in v_copies:
        c.wait()
    await_share(c_one, keys, 2, copies)

    assign(c_one, 2 * head_len, [(HOOKS[1], lambda: w_stage(2, w_step))])
    count_copies = exchange_counts(cr2, 4)
    key_copies = exchange_sums(keys, rs2, 3)
    val_copies = exchange_sums(vals, rs2, 6)
    w_stage(3, w_step)
    for c in count_copies:
        c.wait()
    mass = total_counts(cr2)
    columns(mass)
    count_col = cacc[own_rows, :]
    for c in key_copies:
        c.wait()
    kvc[own_rows, :head_len] = (
        (total_sums(rs2, slice(0, head_len)) + c_one[own_rows, :].astype(jnp.float32))
        / count_col
    ).astype(jnp.bfloat16)
    key_share = share(kvc, keys, 5)
    for c in val_copies:
        c.wait()
    kvc[own_rows, head_len:] = (
        total_sums(rs2, slice(head_len, 2 * head_len)) / count_col
    ).astype(jnp.bfloat16)
    val_share = share(kvc, vals, 7)
    columns(jnp.log(mass).astype(jnp.bfloat16).astype(jnp.float32) * LOG2E)
    lmass[...] = cacc[:, :1]
    q_mine.wait()
    for c in q_copies:
        c.wait()
    await_share(kvc, keys, 5, key_share)

    piece = q_cols // heads

    def member(m):
        return pl.ds(pl.multiple_of(m * piece, piece), piece)

    scale = LOG2E / (float(head_len) ** 0.5)
    early = shard == piece and group_len == heads
    order_of_heads = [mates[2], mates[3], mates[1], j] if early else range(group_len)
    for slot_of, g in enumerate(order_of_heads):
        cols = pl.ds(pl.multiple_of(g * head_len, head_len), head_len)
        scores = lax.dot_general(
            kvc[:, :head_len], qbuf[:, cols], (((1,), (1,)), ((), ())),
            preferred_element_type=jnp.float32,
        )
        scores = scores * scale + lmass[...]
        e = jnp.exp2(scores - jnp.max(scores, axis=0, keepdims=True))
        probs[slot_of] = (e * (1.0 / jnp.sum(e, axis=0, keepdims=True))).astype(jnp.bfloat16)
    await_share(kvc, vals, 7, val_share)
    val_t = kvc[:, head_len:].astype(jnp.float32).T.astype(jnp.bfloat16)

    a_copies = [None] + [
        remote(
            atts.at[:, member(mates[k])], xin.at[:, member(j)],
            psend.at[12 + k], precv.at[12 + k], plane(k),
        )
        for k in (1, 2, 3)
    ]
    a_mine = pltpu.make_async_copy(
        atts.at[:, member(j)], xin.at[:, member(j)], loc_sem.at[3]
    )
    sends = [a_copies[2], a_copies[3], a_copies[1], a_mine]
    for slot_of, g in enumerate(order_of_heads):
        mixed = jnp.dot(val_t, probs[slot_of], preferred_element_type=jnp.float32)
        cols = pl.ds(pl.multiple_of(g * head_len, head_len), head_len)
        atts[:, cols] = mixed.T.astype(jnp.bfloat16)
        if early:
            sends[slot_of].start()
    if not early:
        src = lax.broadcasted_iota(jnp.int32, (q_cols, q_cols), 0)
        dst = lax.broadcasted_iota(jnp.int32, (q_cols, q_cols), 1)
        block = src // shard
        target = (block % heads) * piece + (block // heads) * shard + src % shard
        order = jnp.where(dst == target, 1.0, 0.0).astype(jnp.bfloat16)
        atts[...] = jnp.dot(
            atts[...], order, preferred_element_type=jnp.float32
        ).astype(jnp.bfloat16)

    if not early:
        for c in sends:
            c.start()

    @pl.loop(0, rows_of_line)
    def _(q):
        @pl.when((q <= p) & (p < rows_of_line - 1))
        def _():
            w_copy(q, wr_send.at[q], right).wait_send()

        @pl.when((q >= p) & (p > 0))
        def _():
            w_copy(q, wl_send.at[q], left).wait_send()

        if halves == 2:
            @pl.when(q != p)
            def _():
                twin_arrival(q).wait_recv()
                twin(q).wait_send()

    a_mine.wait()
    for k in (1, 2, 3):
        a_copies[k].wait_send()
        remote(
            atts.at[:, member(mates[k])], xin.at[:, member(mates[k])],
            psend.at[12 + k], precv.at[12 + k], plane(k),
        ).wait_recv()

    width = w_line.shape[1] // COLUMN_TILES

    def block_of(m):
        return pl.ds(pl.multiple_of(m * q_rows, q_rows), q_rows)

    def to_sibling(t):
        return remote(
            sib_out.at[t], sib_in.at[t], tsend.at[0, t], trecv.at[0, t], plane(1)
        )

    def to_chip(t):
        return remote(x_out.at[t], x_in.at[t], tsend.at[1, t], trecv.at[1, t], plane(2))

    def pass_on(t):
        cols = slice(t * width, (t + 1) * width)
        to_sibling(t).wait_recv()
        x_out[t] = (
            yf[block_of(mates[2]), cols] + sib_in[t, q_rows:, :].astype(jnp.float32)
        ).astype(jnp.bfloat16)
        to_chip(t).start()

    for t in range(COLUMN_TILES):
        cols = slice(t * width, (t + 1) * width)
        yf[:, cols] = jnp.dot(xin[...], w_line[:, cols], preferred_element_type=jnp.float32)
        sib_out[t, :q_rows, :] = yf[block_of(mates[1]), cols].astype(jnp.bfloat16)
        sib_out[t, q_rows:, :] = yf[block_of(mates[3]), cols].astype(jnp.bfloat16)
        to_sibling(t).start()
        if t > 0:
            pass_on(t - 1)
    pass_on(COLUMN_TILES - 1)
    for t in range(COLUMN_TILES):
        cols = slice(t * width, (t + 1) * width)
        to_sibling(t).wait_send()
        to_chip(t).wait()
        out_ref[:, cols] = (
            yf[block_of(j), cols]
            + sib_in[t, :q_rows, :].astype(jnp.float32)
            + x_in[t].astype(jnp.float32)
        ).astype(out_ref.dtype)


def per_device(n, halves, kcodes, kscale, vcodes, vscale, seed, softness, questions, weight):
    heads, centres, head_len = seed.shape
    line = n // heads
    tokens = kcodes.shape[0]
    q_rows, q_width = questions.shape
    depth, width = weight.shape
    chunk = centres // line
    bf16, f32 = jnp.bfloat16, jnp.float32
    vm = pltpu.VMEM
    dma = pltpu.SemaphoreType.DMA
    anywhere = pl.BlockSpec(memory_space=pl.ANY)
    scalars = pl.BlockSpec(memory_space=pltpu.SMEM)
    q_cols = q_width // heads
    return pl.pallas_call(
        functools.partial(kernel, line, heads, halves),
        out_shape=jax.ShapeDtypeStruct((q_rows, width), bf16),
        in_specs=[anywhere, scalars, anywhere, scalars, anywhere, scalars, anywhere, anywhere],
        out_specs=pl.BlockSpec(memory_space=pltpu.VMEM),
        scratch_shapes=[
            vm(kcodes.shape, kcodes.dtype),
            vm(vcodes.shape, vcodes.dtype),
            vm(questions.shape, bf16),
            vm((centres, head_len), bf16),
            vm((heads, tokens, head_len), bf16),
            vm((heads, tokens, head_len), bf16),
            vm((heads * tokens, 2 * head_len), bf16),
            vm((heads * q_rows, q_cols), bf16),
            vm((centres, head_len), bf16),
            vm((centres, 2 * head_len), bf16),
            vm((centres, 1), f32),
            vm((centres, 2 * head_len), f32),
            vm((centres, 128), f32),
            vm((centres, 2 * head_len), bf16),
            vm((centres // 128, 128), f32),
            vm((line, chunk, head_len), bf16),
            vm((line, centres // 128, 128), f32),
            vm((line, chunk, 2 * head_len), bf16),
            vm((line, centres // 128, 128), f32),
            vm((centres, 1), f32),
            vm((heads * q_rows, q_cols), bf16),
            vm((heads * q_rows, q_cols), bf16),
            vm((q_cols // head_len, centres, heads * q_rows), bf16),
            vm((line * depth, width), bf16),
            vm((heads * q_rows, width), f32),
            vm((COLUMN_TILES, 2 * q_rows, width // COLUMN_TILES), bf16),
            vm((COLUMN_TILES, 2 * q_rows, width // COLUMN_TILES), bf16),
            vm((COLUMN_TILES, q_rows, width // COLUMN_TILES), bf16),
            vm((COLUMN_TILES, q_rows, width // COLUMN_TILES), bf16),
            dma((5,)),
            dma((4,)),
            dma((16,)),
            dma((16,)),
            dma((8, line)),
            dma((8, line)),
            dma((line,)),
            dma((line,)),
            dma((line,)),
            dma((line,)),
            dma((line,)),
            dma((2, COLUMN_TILES)),
            dma((2, COLUMN_TILES)),
        ],
        compiler_params=pltpu.CompilerParams(
            collective_id=0, has_side_effects=True, vmem_limit_bytes=60 * 1024 * 1024
        ),
    )(kcodes, kscale, vcodes, vscale, seed, softness, questions, weight)


def solution(mesh):
    in_specs = (
        P(("groups", "ctx"), None),
        P(("groups", "ctx"), None),
        P(("groups", "ctx"), None),
        P(("groups", "ctx"), None),
        P("groups", None, None),
        P("groups"),
        P(("groups", "ctx"), None),
        P("ctx", None),
    )
    out_specs = P(("groups", "ctx"), None)
    return jax.shard_map(
        functools.partial(
            per_device, mesh.shape["ctx"], 2 if mesh.shape["groups"] == 2 else 1
        ),
        mesh=mesh, in_specs=in_specs, out_specs=out_specs, check_vma=False,
    )
```

```python
import functools

import jax
import jax.numpy as jnp
from jax import lax
from jax.experimental import pallas as pl
from jax.experimental.pallas import tpu as pltpu
from jax.sharding import PartitionSpec as P

MESH = pl.DeviceIdType.MESH
LOG2E = 1.4426950408889634
TOKEN_TILE = 256
HOOKS = (4, 0)

COLUMN_TILES = 8


def mate(j, k):
    if k == 1:
        return j + 1 - 2 * lax.rem(j, 2)
    if k == 2:
        return lax.rem(j + 2, 4)
    return 3 - j


def kernel(
    rows_of_line, heads, halves,
    kcodes_hbm, kscale, vcodes_hbm, vscale, seed_hbm, softness, q_hbm, w_hbm,
    out_ref,
    kcodes, vcodes, qin, seed, kst, vst, kv, qbuf, c_one, kvc, csq,
    acc, cacc, sums, cnt, rs1, cr1, rs2, cr2, lmass, atts, xin, probs, w_line, yf, sib_out, sib_in, x_out, x_in,
    load_sem, loc_sem, psend, precv, rsend, rrecv,
    wr_send, wl_send, wy_send, wrecv, wyrecv, tsend, trecv,
):
    n = rows_of_line * heads
    me = lax.axis_index("ctx")
    p, j = lax.div(me, heads), lax.rem(me, heads)
    mates = [None] + [mate(j, k) for k in (1, 2, 3)]
    tokens = kcodes.shape[0]
    head_len = seed.shape[1]
    centres = seed.shape[0]
    chunk = centres // rows_of_line
    shard = w_hbm.shape[0]
    q_rows = qin.shape[0]
    q_cols = qin.shape[1] // heads
    group_len = q_cols // head_len

    def plane(k):
        return p * heads + mates[k]

    def line(k):
        return lax.rem(p + k, rows_of_line) * heads + j

    def remote(src, dst, ss, rs, dev):
        return pltpu.make_async_remote_copy(
            src_ref=src, dst_ref=dst, send_sem=ss, recv_sem=rs,
            device_id={"ctx": dev}, device_id_type=MESH,
        )

    loads = [
        pltpu.make_async_copy(kcodes_hbm, kcodes, load_sem.at[0]),
        pltpu.make_async_copy(vcodes_hbm, vcodes, load_sem.at[1]),
        pltpu.make_async_copy(q_hbm, qin, load_sem.at[2]),
        pltpu.make_async_copy(seed_hbm.at[j], seed, load_sem.at[3]),
    ]
    for item in loads:
        item.start()

    half = w_hbm.shape[1] // halves
    group = lax.axis_index("groups")
    ours = pl.multiple_of((group if halves == 2 else 0) * half, half)
    w_cols = pl.ds(ours, half)

    def w_part(q):
        return w_line.at[pl.ds(pl.multiple_of(q * shard, shard), shard), w_cols]

    own_w = pltpu.make_async_copy(
        w_hbm, w_line.at[pl.ds(pl.multiple_of(p * shard, shard), shard), :], load_sem.at[4]
    )
    own_w.start()

    barrier = pltpu.get_barrier_semaphore()
    for k in (1, 2, 3):
        pl.semaphore_signal(barrier, inc=1, device_id={"ctx": plane(k)}, device_id_type=MESH)
    for k in range(1, rows_of_line):
        pl.semaphore_signal(barrier, inc=1, device_id={"ctx": line(k)}, device_id_type=MESH)
    if halves == 2:
        pl.semaphore_signal(
            barrier, inc=1, device_id={"groups": 1 - group, "ctx": me}, device_id_type=MESH
        )
    pl.semaphore_wait(barrier, 3 + rows_of_line - 1 + halves - 1)

    right = jnp.minimum(p + 1, rows_of_line - 1) * heads + j
    left = jnp.maximum(p - 1, 0) * heads + j

    def w_copy(q, ss, dev):
        return remote(w_part(q), w_part(q), ss, wrecv.at[q], dev)

    def twin(q):
        return pltpu.make_async_remote_copy(
            src_ref=w_part(q), dst_ref=w_part(q), send_sem=wy_send.at[q],
            recv_sem=wyrecv.at[q], device_id={"groups": 1 - group, "ctx": me},
            device_id_type=MESH,
        )

    def twin_arrival(q):
        there = pl.ds(pl.multiple_of((1 - group) * half, half), half)
        part = w_line.at[pl.ds(pl.multiple_of(q * shard, shard), shard), there]
        return pltpu.make_async_remote_copy(
            src_ref=part, dst_ref=part, send_sem=wy_send.at[q],
            recv_sem=wyrecv.at[q], device_id={"groups": 1 - group, "ctx": me},
            device_id_type=MESH,
        )

    def w_step(k):
        lo, hi = p - k, p + k

        @pl.when(lo >= 0)
        def _():
            q = jnp.maximum(lo, 0)
            w_copy(q, wr_send.at[q], right).wait_recv()

            @pl.when(p < rows_of_line - 1)
            def _():
                w_copy(q, wr_send.at[q], right).start()

            if halves == 2:
                twin(q).start()

        @pl.when(hi < rows_of_line)
        def _():
            q = jnp.minimum(hi, rows_of_line - 1)
            w_copy(q, wl_send.at[q], left).wait_recv()

            @pl.when(p > 0)
            def _():
                w_copy(q, wl_send.at[q], left).start()

            if halves == 2:
                twin(q).start()

    def w_stage(stage, step):
        first, last = stage * rows_of_line // 4, (stage + 1) * rows_of_line // 4
        if last - first <= 2:
            for k in range(first, last):
                if k > 0:
                    step(k)
        else:
            @pl.loop(max(first, 1), last)
            def _(k):
                step(k)

    def dequantize(codes, scale, stage, lane, base):
        block = tokens // scale.shape[0]
        for h in range(heads):
            for b in range(scale.shape[0]):
                piece = codes[b * block:(b + 1) * block, h * head_len:(h + 1) * head_len]
                stage[h, b * block:(b + 1) * block, :] = (
                    piece.astype(jnp.float32) * scale[b, h]
                ).astype(jnp.bfloat16)
        cols = pl.ds(lane * head_len, head_len)
        mine = pltpu.make_async_copy(
            stage.at[j], kv.at[pl.ds(0, tokens), cols], loc_sem.at[lane]
        )
        mine.start()
        copies = [
            remote(
                stage.at[mates[k]], kv.at[pl.ds(k * tokens, tokens), cols],
                psend.at[base + k], precv.at[base + k], plane(k),
            )
            for k in (1, 2, 3)
        ]
        for c in copies:
            c.start()
        return mine, copies

    own_w.wait()

    @pl.when(p < rows_of_line - 1)
    def _():
        w_copy(p, wr_send.at[p], right).start()

    @pl.when(p > 0)
    def _():
        w_copy(p, wl_send.at[p], left).start()

    loads[0].wait()
    k_mine, k_copies = dequantize(kcodes, kscale, kst, 0, 0)

    loads[1].wait()
    v_mine, v_copies = dequantize(vcodes, vscale, vst, 1, 4)
    loads[2].wait()
    own_queries = pl.ds(pl.multiple_of(j * q_rows, q_rows), q_rows)
    q_mine = pltpu.make_async_copy(
        qin.at[:, pl.ds(pl.multiple_of(j * q_cols, q_cols), q_cols)],
        qbuf.at[own_queries, :], loc_sem.at[2],
    )
    q_mine.start()
    q_copies = [
        remote(
            qin.at[:, pl.ds(pl.multiple_of(mates[k] * q_cols, q_cols), q_cols)],
            qbuf.at[own_queries, :],
            psend.at[8 + k], precv.at[8 + k], plane(k),
        )
        for k in (1, 2, 3)
    ]
    for c in q_copies:
        c.start()
    loads[3].wait()

    factor = LOG2E / softness[j]

    def assign(centre, width, hooks):
        cf = centre[...].astype(jnp.float32)
        csq[...] = jnp.sum(cf * cf, axis=1, keepdims=True) * factor
        acc[:, :width] = jnp.zeros((centres, width), jnp.float32)
        cacc[...] = jnp.zeros_like(cacc)

        def tile(i):
            rows = pl.ds(pl.multiple_of(i * TOKEN_TILE, TOKEN_TILE), TOKEN_TILE)
            logits = lax.dot_general(
                centre[...], kv[rows, :head_len], (((1,), (1,)), ((), ())),
                preferred_element_type=jnp.float32,
            )
            logits = logits * (2.0 * factor) - csq[...]
            e = jnp.exp2(logits - jnp.max(logits, axis=0, keepdims=True))
            weights = e * (1.0 / jnp.sum(e, axis=0, keepdims=True))
            part = weights[:, :128]
            for s in range(128, TOKEN_TILE, 128):
                part = part + weights[:, s:s + 128]
            cacc[...] += part
            acc[:, :width] += jnp.dot(
                weights.astype(jnp.bfloat16), kv[rows, :width],
                preferred_element_type=jnp.float32,
            )

        tiles = heads * tokens // TOKEN_TILE
        stops = sorted({0, tiles, *(at for at, _ in hooks)})
        for first, last in zip(stops, stops[1:]):
            for at, hook in hooks:
                if at == first:
                    hook()
            pl.loop(first, last)(tile)
        sums[:, :width] = acc[:, :width].astype(jnp.bfloat16)
        for b in range(centres // 128):
            cnt[b:b + 1, :] = jnp.sum(
                cacc[b * 128:(b + 1) * 128, :].T, axis=0, keepdims=True
            )

    keys, vals = pl.ds(0, head_len), pl.ds(head_len, head_len)

    def exchange_sums(lanes, rs, base):
        copies = []
        for k in range(1, rows_of_line):
            rows = pl.ds(pl.multiple_of(lax.rem(p + k, rows_of_line) * chunk, chunk), chunk)
            copies.append(remote(
                sums.at[rows, lanes], rs.at[k, :, lanes],
                rsend.at[base, k], rrecv.at[base, k], line(k),
            ))
        for c in copies:
            c.start()
        return copies

    def exchange_counts(cr, base):
        copies = [
            remote(cnt, cr.at[k], rsend.at[base, k], rrecv.at[base, k], line(k))
            for k in range(1, rows_of_line)
        ]
        for c in copies:
            c.start()
        return copies

    def total_counts(cr):
        total = cnt[...]
        for k in range(1, rows_of_line):
            total = total + cr[k]
        return total + 1.0

    def columns(rows8):
        for b in range(centres // 128):
            cacc[b * 128:(b + 1) * 128, :] = jnp.broadcast_to(rows8[b:b + 1, :], (128, 128)).T

    own_rows = pl.ds(pl.multiple_of(p * chunk, chunk), chunk)

    def total_sums(rs, lanes):
        total = acc[own_rows, lanes]
        for k in range(1, rows_of_line):
            total = total + rs[k, :, lanes].astype(jnp.float32)
        return total

    def share(buf, lanes, base):
        copies = [
            remote(buf.at[own_rows, lanes], buf.at[own_rows, lanes],
                   rsend.at[base, k], rrecv.at[base, k], line(k))
            for k in range(1, rows_of_line)
        ]
        for c in copies:
            c.start()
        return copies

    def await_share(buf, lanes, base, copies):
        for k in range(1, rows_of_line):
            copies[k - 1].wait_send()
            q = lax.rem(p + rows_of_line - k, rows_of_line)
            rows = pl.ds(pl.multiple_of(q * chunk, chunk), chunk)
            remote(buf.at[rows, lanes], buf.at[rows, lanes],
                   rsend.at[base, k], rrecv.at[base, k], line(k)).wait_recv()

    slot = tokens // TOKEN_TILE
    assign(seed, head_len, [
        (0, k_mine.wait), (slot, k_copies[0].wait),
        (2 * slot, k_copies[1].wait), (3 * slot, k_copies[2].wait),
        (HOOKS[0], lambda: (w_stage(0, w_step), w_stage(1, w_step))),
    ])
    copies = exchange_counts(cr1, 1) + exchange_sums(keys, rs1, 0)
    for c in copies:
        c.wait()
    columns(total_counts(cr1))
    c_one[own_rows, :] = (
        (total_sums(rs1, slice(0, head_len)) + seed[own_rows, :].astype(jnp.float32))
        / cacc[own_rows, :]
    ).astype(jnp.bfloat16)
    copies = share(c_one, keys, 2)
    w_stage(2, w_step)
    v_mine.wait()
    for c in v_copies:
        c.wait()
    await_share(c_one, keys, 2, copies)

    assign(c_one, 2 * head_len, [])
    count_copies = exchange_counts(cr2, 4)
    key_copies = exchange_sums(keys, rs2, 3)
    val_copies = exchange_sums(vals, rs2, 6)
    w_stage(3, w_step)
    for c in count_copies:
        c.wait()
    mass = total_counts(cr2)
    columns(mass)
    count_col = cacc[own_rows, :]
    for c in key_copies:
        c.wait()
    kvc[own_rows, :head_len] = (
        (total_sums(rs2, slice(0, head_len)) + c_one[own_rows, :].astype(jnp.float32))
        / count_col
    ).astype(jnp.bfloat16)
    key_share = share(kvc, keys, 5)
    for c in val_copies:
        c.wait()
    kvc[own_rows, head_len:] = (
        total_sums(rs2, slice(head_len, 2 * head_len)) / count_col
    ).astype(jnp.bfloat16)
    val_share = share(kvc, vals, 7)
    columns(jnp.log(mass).astype(jnp.bfloat16).astype(jnp.float32) * LOG2E)
    lmass[...] = cacc[:, :1]
    q_mine.wait()
    for c in q_copies:
        c.wait()
    await_share(kvc, keys, 5, key_share)

    piece = q_cols // heads

    def member(m):
        return pl.ds(pl.multiple_of(m * piece, piece), piece)

    scale = LOG2E / (float(head_len) ** 0.5)
    early = shard == piece and group_len == heads
    order_of_heads = [mates[2], mates[3], mates[1], j] if early else range(group_len)
    for slot_of, g in enumerate(order_of_heads):
        cols = pl.ds(pl.multiple_of(g * head_len, head_len), head_len)
        scores = lax.dot_general(
            kvc[:, :head_len], qbuf[:, cols], (((1,), (1,)), ((), ())),
            preferred_element_type=jnp.float32,
        )
        scores = scores * scale + lmass[...]
        e = jnp.exp2(scores - jnp.max(scores, axis=0, keepdims=True))
        probs[slot_of] = (e * (1.0 / jnp.sum(e, axis=0, keepdims=True))).astype(jnp.bfloat16)
    await_share(kvc, vals, 7, val_share)
    val_t = kvc[:, head_len:].astype(jnp.float32).T.astype(jnp.bfloat16)

    a_copies = [None] + [
        remote(
            atts.at[:, member(mates[k])], xin.at[:, member(j)],
            psend.at[12 + k], precv.at[12 + k], plane(k),
        )
        for k in (1, 2, 3)
    ]
    a_mine = pltpu.make_async_copy(
        atts.at[:, member(j)], xin.at[:, member(j)], loc_sem.at[3]
    )
    sends = [a_copies[2], a_copies[3], a_copies[1], a_mine]
    for slot_of, g in enumerate(order_of_heads):
        mixed = jnp.dot(val_t, probs[slot_of], preferred_element_type=jnp.float32)
        cols = pl.ds(pl.multiple_of(g * head_len, head_len), head_len)
        atts[:, cols] = mixed.T.astype(jnp.bfloat16)
        if early:
            sends[slot_of].start()
    if not early:
        src = lax.broadcasted_iota(jnp.int32, (q_cols, q_cols), 0)
        dst = lax.broadcasted_iota(jnp.int32, (q_cols, q_cols), 1)
        block = src // shard
        target = (block % heads) * piece + (block // heads) * shard + src % shard
        order = jnp.where(dst == target, 1.0, 0.0).astype(jnp.bfloat16)
        atts[...] = jnp.dot(
            atts[...], order, preferred_element_type=jnp.float32
        ).astype(jnp.bfloat16)

    if not early:
        for c in sends:
            c.start()

    @pl.loop(0, rows_of_line)
    def _(q):
        @pl.when((q <= p) & (p < rows_of_line - 1))
        def _():
            w_copy(q, wr_send.at[q], right).wait_send()

        @pl.when((q >= p) & (p > 0))
        def _():
            w_copy(q, wl_send.at[q], left).wait_send()

        if halves == 2:
            @pl.when(q != p)
            def _():
                twin_arrival(q).wait_recv()
                twin(q).wait_send()

    a_mine.wait()
    for k in (1, 2, 3):
        a_copies[k].wait_send()
        remote(
            atts.at[:, member(mates[k])], xin.at[:, member(mates[k])],
            psend.at[12 + k], precv.at[12 + k], plane(k),
        ).wait_recv()

    width = w_line.shape[1] // COLUMN_TILES

    def block_of(m):
        return pl.ds(pl.multiple_of(m * q_rows, q_rows), q_rows)

    def to_sibling(t):
        return remote(
            sib_out.at[t], sib_in.at[t], tsend.at[0, t], trecv.at[0, t], plane(1)
        )

    def to_chip(t):
        return remote(x_out.at[t], x_in.at[t], tsend.at[1, t], trecv.at[1, t], plane(2))

    def pass_on(t):
        cols = slice(t * width, (t + 1) * width)
        to_sibling(t).wait_recv()
        x_out[t] = (
            yf[block_of(mates[2]), cols] + sib_in[t, q_rows:, :].astype(jnp.float32)
        ).astype(jnp.bfloat16)
        to_chip(t).start()

    for t in range(COLUMN_TILES):
        cols = slice(t * width, (t + 1) * width)
        yf[:, cols] = jnp.dot(xin[...], w_line[:, cols], preferred_element_type=jnp.float32)
        sib_out[t, :q_rows, :] = yf[block_of(mates[1]), cols].astype(jnp.bfloat16)
        sib_out[t, q_rows:, :] = yf[block_of(mates[3]), cols].astype(jnp.bfloat16)
        to_sibling(t).start()
        if t > 0:
            pass_on(t - 1)
    pass_on(COLUMN_TILES - 1)
    for t in range(COLUMN_TILES):
        cols = slice(t * width, (t + 1) * width)
        to_sibling(t).wait_send()
        to_chip(t).wait()
        out_ref[:, cols] = (
            yf[block_of(j), cols]
            + sib_in[t, :q_rows, :].astype(jnp.float32)
            + x_in[t].astype(jnp.float32)
        ).astype(out_ref.dtype)


def per_device(n, halves, kcodes, kscale, vcodes, vscale, seed, softness, questions, weight):
    heads, centres, head_len = seed.shape
    line = n // heads
    tokens = kcodes.shape[0]
    q_rows, q_width = questions.shape
    depth, width = weight.shape
    chunk = centres // line
    bf16, f32 = jnp.bfloat16, jnp.float32
    vm = pltpu.VMEM
    dma = pltpu.SemaphoreType.DMA
    anywhere = pl.BlockSpec(memory_space=pl.ANY)
    scalars = pl.BlockSpec(memory_space=pltpu.SMEM)
    q_cols = q_width // heads
    return pl.pallas_call(
        functools.partial(kernel, line, heads, halves),
        out_shape=jax.ShapeDtypeStruct((q_rows, width), bf16),
        in_specs=[anywhere, scalars, anywhere, scalars, anywhere, scalars, anywhere, anywhere],
        out_specs=pl.BlockSpec(memory_space=pltpu.VMEM),
        scratch_shapes=[
            vm(kcodes.shape, kcodes.dtype),
            vm(vcodes.shape, vcodes.dtype),
            vm(questions.shape, bf16),
            vm((centres, head_len), bf16),
            vm((heads, tokens, head_len), bf16),
            vm((heads, tokens, head_len), bf16),
            vm((heads * tokens, 2 * head_len), bf16),
            vm((heads * q_rows, q_cols), bf16),
            vm((centres, head_len), bf16),
            vm((centres, 2 * head_len), bf16),
            vm((centres, 1), f32),
            vm((centres, 2 * head_len), f32),
            vm((centres, 128), f32),
            vm((centres, 2 * head_len), bf16),
            vm((centres // 128, 128), f32),
            vm((line, chunk, head_len), bf16),
            vm((line, centres // 128, 128), f32),
            vm((line, chunk, 2 * head_len), bf16),
            vm((line, centres // 128, 128), f32),
            vm((centres, 1), f32),
            vm((heads * q_rows, q_cols), bf16),
            vm((heads * q_rows, q_cols), bf16),
            vm((q_cols // head_len, centres, heads * q_rows), bf16),
            vm((line * depth, width), bf16),
            vm((heads * q_rows, width), f32),
            vm((COLUMN_TILES, 2 * q_rows, width // COLUMN_TILES), bf16),
            vm((COLUMN_TILES, 2 * q_rows, width // COLUMN_TILES), bf16),
            vm((COLUMN_TILES, q_rows, width // COLUMN_TILES), bf16),
            vm((COLUMN_TILES, q_rows, width // COLUMN_TILES), bf16),
            dma((5,)),
            dma((4,)),
            dma((16,)),
            dma((16,)),
            dma((8, line)),
            dma((8, line)),
            dma((line,)),
            dma((line,)),
            dma((line,)),
            dma((line,)),
            dma((line,)),
            dma((2, COLUMN_TILES)),
            dma((2, COLUMN_TILES)),
        ],
        compiler_params=pltpu.CompilerParams(
            collective_id=0, has_side_effects=True, vmem_limit_bytes=60 * 1024 * 1024
        ),
    )(kcodes, kscale, vcodes, vscale, seed, softness, questions, weight)


def solution(mesh):
    in_specs = (
        P(("groups", "ctx"), None),
        P(("groups", "ctx"), None),
        P(("groups", "ctx"), None),
        P(("groups", "ctx"), None),
        P("groups", None, None),
        P("groups"),
        P(("groups", "ctx"), None),
        P("ctx", None),
    )
    out_specs = P(("groups", "ctx"), None)
    return jax.shard_map(
        functools.partial(
            per_device, mesh.shape["ctx"], 2 if mesh.shape["groups"] == 2 else 1
        ),
        mesh=mesh, in_specs=in_specs, out_specs=out_specs, check_vma=False,
    )
```
